32 devices in a mesh: row: 4 (over z), col: 8 (over y, x, core).
Axes of the slice: x: 2, y: 2, z: 4, core: 2. Of those that a mesh axis runs over, the one named last changes fastest.
Arguments:
- activations: bfloat16 [4096, 4096], P('col', 'row'), may hold values from -6 to 6
- out_grads: bfloat16 [4096, 2048], P('row', 'col'), may hold values from -0.09375 to 0.09375
- statistics: float32 [4, 8, 512, 1024], P('row', 'col'), may hold values from -10 to 200, as said below
Outputs:
- new_statistics: float32 [4, 8, 512, 1024], P('row', 'col')
- update: bfloat16 [4096, 2048], P('row', 'col')
The draws below stay inside these ranges and needn't reach their ends.
Inputs may be any that keep to these rules, and one draw needn't show every extreme that they name: `statistics`: every statistic is symmetric and positive definite.
All inputs are finite; a program needn't handle non-finite values.
Results may differ from the reference program's by a relative error of at most 0.0017.
The reference program's roundings to bfloat16 on the way count: a program that leaves them out, or rounds other values in their place, can miss the bound.
Values may be sent and summed in bfloat16 or wider, within the bound.
A program may use at most 128 MiB of HBM per device.

```python
import math
import jax
import jax.numpy as jnp
from jax import lax

BLOCK = 1024
ITERS = 2
DAMP_EXP = 3
TOKENS = 4096
D_IN = 4096
D_OUT = 2048


def draw_statistics(key, part):
    in_count = D_IN // BLOCK
    out_count = D_OUT // BLOCK
    stat_count = in_count * out_count * 2
    noise_key, diagonal_key, scale_key = jax.random.split(jax.random.fold_in(key, 17), 3)
    noise_draw = jax.random.normal(noise_key, (stat_count, BLOCK, BLOCK), jnp.float32)
    symmetric = (noise_draw + jnp.swapaxes(noise_draw, 1, 2)) * (0.70710678 / 80.0)
    diagonal = jax.random.uniform(diagonal_key, (stat_count, BLOCK), jnp.float32, 1.0, 2.0)
    upper_scale = 3.0
    scales = jnp.exp(jax.random.uniform(scale_key, (stat_count, BLOCK), jnp.float32, 0.0, math.log(upper_scale)))
    identity = jnp.eye(BLOCK, dtype=jnp.float32)
    base_matrix = symmetric * (1.0 - identity)[None] + identity[None] * diagonal[:, :, None]
    full_stats = scales[:, :, None] * base_matrix * scales[:, None, :]
    full_stats = full_stats.reshape(in_count, out_count, 2, 2, BLOCK // 2, BLOCK).transpose(0, 1, 3, 2, 4, 5)
    return full_stats.reshape(in_count, 4 * out_count, BLOCK // 2, BLOCK)


def block_scale(key, dims, cuts, low, high):
    gain, own = 1.0, jax.random.fold_in(key, 6)
    for dim, blocks in cuts:
        steps = jnp.exp(jax.random.uniform(jax.random.fold_in(own, dim), (blocks,), jnp.float32, low / len(cuts), high / len(cuts)))
        gain = gain * jnp.repeat(steps, dims[dim] // blocks).reshape([-1 if axis == dim else 1 for axis in range(len(dims))])
    return gain


def normal_values(rng, shape, scale, most, cuts=(), kind=jnp.bfloat16):
    values = scale * jax.random.normal(rng, shape, jnp.float32)
    if cuts:
        values = values * block_scale(rng, shape, cuts, -0.22, 0.18)
    return jnp.clip(values, -most, most).astype(kind)


def setup_inputs(seed: int = 0) -> dict:
    key_list = jax.random.split(jax.random.key(seed), 4)
    activations = normal_values(key_list[0], (TOKENS, D_IN), 1.0, 6.0, ((0, 8), (1, 4)))
    out_grads = normal_values(key_list[1], (TOKENS, D_OUT), TOKENS ** -0.5, 0.09375, ((0, 4), (1, 8)))
    statistics = draw_statistics(jax.random.fold_in(key_list[3], 71), 0)
    return dict(activations=activations, out_grads=out_grads, statistics=statistics)


DECAY = 0.9
EPS = 1e-06

def matmul_high(left, right):
    return jnp.dot(left, right, precision=lax.Precision.HIGHEST, preferred_element_type=jnp.float32)

def inverse_root(statistic):
    matrix_order = statistic.shape[0]
    identity = jnp.eye(matrix_order, dtype=jnp.float32)
    damping = 10.0 ** (-DAMP_EXP) * jnp.trace(statistic) / matrix_order
    damped = statistic + damping * identity
    scaling = jnp.max(lax.optimization_barrier(jnp.sum(jnp.abs(damped), axis=1))) / 4.0
    normed = damped / scaling
    result = identity
    for iteration in range(ITERS):
        factor = (5.0 * identity - normed) / 4.0
        if iteration == 0:
            result = factor
        else:
            result = matmul_high(result, factor)
        if iteration + 1 < ITERS:
            square = matmul_high(factor, factor)
            fourth = matmul_high(square, square)
            normed = matmul_high(fourth, normed)
    return result

def one_block(block_item):
    grad_block, old_pair = block_item
    left_gram = jnp.dot(grad_block, grad_block.T, preferred_element_type=jnp.float32)
    right_gram = jnp.dot(grad_block.T, grad_block, preferred_element_type=jnp.float32)
    renewed = jnp.stack([DECAY * old_pair[0] + (1.0 - DECAY) / BLOCK * left_gram, DECAY * old_pair[1] + (1.0 - DECAY) / BLOCK * right_gram])
    left_root = inverse_root(old_pair[0]).astype(jnp.bfloat16)
    right_root = inverse_root(old_pair[1]).astype(jnp.bfloat16)
    half_product = jnp.dot(grad_block, right_root, preferred_element_type=jnp.float32).astype(jnp.bfloat16)
    conditioned = jnp.dot(left_root, half_product, preferred_element_type=jnp.float32)
    column_tiles = conditioned.reshape(BLOCK, 4, BLOCK // 4)
    grad_tiles = grad_block.astype(jnp.float32).reshape(BLOCK, 4, BLOCK // 4)
    grad_power = lax.optimization_barrier(jnp.mean(grad_tiles * grad_tiles, axis=(0, 2)))
    cond_power = lax.optimization_barrier(jnp.mean(column_tiles * column_tiles, axis=(0, 2)))
    graft_ratio = jnp.sqrt(grad_power / (cond_power + EPS))
    update = (column_tiles * graft_ratio[None, :, None]).reshape(BLOCK, BLOCK).astype(jnp.bfloat16)
    return (renewed, update)

def reference(activations, out_grads, statistics):
    gradient = jnp.dot(activations.T, out_grads, preferred_element_type=jnp.float32).astype(jnp.bfloat16)
    in_count = D_IN // BLOCK
    out_count = D_OUT // BLOCK
    grad_blocks = gradient.reshape(in_count, BLOCK, out_count, BLOCK).transpose(0, 2, 1, 3).reshape(-1, BLOCK, BLOCK)
    previous = statistics.reshape(in_count, out_count, 2, 2, BLOCK // 2, BLOCK).transpose(0, 1, 3, 2, 4, 5)
    previous = previous.reshape(in_count * out_count, 2, BLOCK, BLOCK)
    renewed, updates = lax.map(one_block, (grad_blocks, previous))
    new_statistics = renewed.reshape(in_count, out_count, 2, 2, BLOCK // 2, BLOCK).transpose(0, 1, 3, 2, 4, 5)
    new_statistics = new_statistics.reshape(in_count, 4 * out_count, BLOCK // 2, BLOCK)
    update = updates.reshape(in_count, out_count, BLOCK, BLOCK).transpose(0, 2, 1, 3).reshape(D_IN, D_OUT)
    return (new_statistics, update)
```

```python
import jax
import jax.numpy as jnp
from jax import lax
from jax.sharding import PartitionSpec as P

DAMP_EXP = 3
DECAY = 0.9
EPS = 1e-06


def from_partner(block, axis, stride):
    count = lax.axis_size(axis)
    route = []
    for low in range(count):
        high = low | 1 << stride
        if high != low and high < count:
            route += [(low, high), (high, low)]
    return lax.ppermute(block, axis, route)


def shifted(block, axis, step):
    count = lax.axis_size(axis)
    return lax.ppermute(block, axis, [(src, (src + step) % count) for src in range(count)])


def product(left, right, over=((1,), (0,)), precision=None):
    return lax.dot_general(
        left, right, (over, ((), ())), precision=precision, preferred_element_type=jnp.float32
    )


def by_half(own, other, own_first, dim):
    first = jnp.where(own_first, own, other)
    second = jnp.where(own_first, other, own)
    return jnp.concatenate([first, second], dim)


def cut(array, index, size, dim):
    return lax.dynamic_slice_in_dim(array, index * size, size, dim)


def half_root(own_diag, own_off, other_diag):
    half = own_diag.shape[0]
    order = 2 * half
    own_rows = jnp.sum(jnp.abs(own_diag), axis=1) + jnp.sum(jnp.abs(own_off), axis=1)
    other_rows = jnp.sum(jnp.abs(other_diag), axis=1) + jnp.sum(jnp.abs(own_off), axis=0)
    eye = jnp.eye(half, dtype=jnp.float32)
    trace = jnp.sum(own_diag * eye) + jnp.sum(other_diag * eye)
    damping = 10.0 ** (-DAMP_EXP) * trace / order
    scaling = (jnp.maximum(jnp.max(own_rows), jnp.max(other_rows)) + damping) / 4.0
    scale = 0.25 / scaling
    top = jnp.concatenate([own_diag, own_off], 1)
    bottom = jnp.concatenate([own_off.T, other_diag], 1)
    damped = jnp.concatenate([top, bottom], 0)
    factor = (1.25 - damping * scale) * jnp.eye(order, dtype=jnp.float32) - damped * scale
    high = lax.Precision.HIGH
    square = product(factor, factor, precision=high)
    fourth = product(square[:half], square, precision=high)
    rest = product(fourth, 5.0 * factor - 4.0 * square, precision=high)
    return (5.0 * factor[:half] - rest) / 4.0


def local(activations, out_grads, statistics):
    half = statistics.shape[2]
    order = statistics.shape[3]
    piece = activations.shape[0]
    width = out_grads.shape[1]
    column = lax.axis_index("col")
    side = column % 2
    half_index = column // 2 % 2
    own_first = half_index == 0
    own_stat = statistics[0, 0]

    own_pieces = [activations]
    stride = 1
    while 1 << stride < lax.axis_size("col"):
        own_pieces += [from_partner(part, "col", stride) for part in own_pieces]
        if stride == 1:
            own_diag = cut(own_stat, half_index, half, 1)
            own_off = cut(own_stat, 1 - half_index, half, 1)
            other_diag = from_partner(own_diag, "col", 1)
        stride += 1

    kept = cut(out_grads, side, piece, 0)
    sent = cut(out_grads, 1 - side, piece, 0)
    sibling = from_partner(sent, "col", 0)
    grads_here = by_half(kept, sibling, side == 0, 1)
    row = lax.axis_index("row")
    row_count = lax.axis_size("row")
    all_grads = jnp.stack(
        [grads_here] + [shifted(grads_here, "row", step) for step in range(1, row_count)]
    )

    root = half_root(own_diag, own_off, other_diag).astype(jnp.bfloat16)
    root_sibling = from_partner(root, "col", 0)
    left_half = jnp.where(side == 0, root, root_sibling)
    right_half = jnp.where(side == 0, root_sibling, root)
    left_own, left_off = left_half[:, :half], left_half[:, half:]
    left_other = from_partner(left_own, "col", 1)
    right_rows = cut(right_half, side, width, 0)

    partial = None
    for index, part in enumerate(own_pieces):
        source = (column // 2) ^ index
        step = (row - source) % row_count
        grads = lax.dynamic_index_in_dim(all_grads, step, 0, keepdims=False)
        term = product(part, grads, ((0,), (0,)))
        partial = term if partial is None else partial + term
    tile_sum = cut(partial, side, width, 1) + from_partner(
        cut(partial, 1 - side, width, 1), "col", 0
    )
    tile = tile_sum.astype(jnp.bfloat16)
    pair_own = by_half(tile, from_partner(tile, "col", 0), side == 0, 1)
    far_tile = from_partner(tile, "col", 1)
    pair_other = by_half(far_tile, from_partner(far_tile, "col", 0), side == 0, 1)

    half_product = (
        product(pair_own, right_rows[:, :half], ((1,), (1,)))
        + product(pair_other, right_rows[:, half:], ((1,), (1,)))
    ).astype(jnp.bfloat16)
    hp_own = cut(half_product, half_index, half, 0)
    hp_other = cut(half_product, 1 - half_index, half, 0)
    cond_own = product(left_own, hp_own) + product(left_off, hp_other)
    cond_other = product(left_off, hp_own, ((0,), (0,))) + product(left_other, hp_other)
    grad_values = tile.astype(jnp.float32)
    count = order * width
    cond_power = (jnp.sum(cond_own * cond_own) + jnp.sum(cond_other * cond_other)) / count
    ratio = jnp.sqrt(jnp.mean(grad_values * grad_values) / (cond_power + EPS))
    update = by_half(
        (cond_own * ratio).astype(jnp.bfloat16),
        (cond_other * ratio).astype(jnp.bfloat16),
        own_first,
        0,
    )

    def left_gram():
        return product(cut(pair_own, half_index, half, 0), pair_own, ((1,), (1,))) + product(
            cut(pair_other, half_index, half, 0), pair_other, ((1,), (1,))
        )

    def right_gram():
        mine = product(pair_own, pair_own, ((0,), (0,)))
        cross = product(pair_own, pair_other, ((0,), (0,)))
        return by_half(mine, cross, own_first, 1)

    gram = lax.cond(side == 0, left_gram, right_gram)
    renewed = DECAY * own_stat + (1.0 - DECAY) / order * gram
    return (renewed[None, None], update)


def solution(mesh):
    placed = (P("col", "row"), P("row", "col"), P("row", "col", None, None))
    return jax.shard_map(
        local,
        mesh=mesh,
        in_specs=placed,
        out_specs=(P("row", "col", None, None), P("row", "col")),
        check_vma=False,
    )
```

```python
import functools

import jax
import jax.numpy as jnp
from jax import lax
from jax.experimental import pallas as pl
from jax.experimental.pallas import tpu as pltpu
from jax.sharding import PartitionSpec as P

DAMP_EXP = 3
DECAY = 0.9
EPS = 1e-06

F32 = jnp.float32
BF16 = jnp.bfloat16


def product(left, right, over=((1,), (0,))):
    return lax.dot_general(left, right, (over, ((), ())), preferred_element_type=F32)


def split(value):
    high = value.astype(BF16)
    return high, (value - high.astype(F32)).astype(BF16)


def total(value):
    return jnp.sum(jnp.sum(value, axis=1, keepdims=True), axis=0, keepdims=True)


def flip(index, bit):
    return index + (1 - 2 * (index // (1 << bit) % 2)) * (1 << bit)


def shampoo_kernel(
    rows,
    cols,
    act,
    og,
    stat,
    renewed,
    update,
    acts,
    grads,
    partial,
    from_sibling,
    pair_own,
    pair_other,
    other_diag,
    f_hi,
    f_lo,
    q_hi,
    q_lo,
    w_hi,
    w_lo,
    p_hi,
    p_lo,
    root,
    root_sibling,
    left,
    left_other,
    hp,
    send_sem,
    recv_sem,
    local_sem,
):
    row = lax.axis_index("row")
    col = lax.axis_index("col")
    side = col % 2
    half_index = col // 2 % 2
    half, order = stat.shape
    piece = act.shape[0]
    width = og.shape[1]
    pieces = cols // 2
    bits = pieces.bit_length() - 1
    block = min(256, half)
    used = [0]

    def at_col(bit):
        return (row, flip(col, bit))

    def send(src, dst, device):
        slot = used[0]
        used[0] += 1
        copy = pltpu.make_async_remote_copy(
            src_ref=src,
            dst_ref=dst,
            send_sem=send_sem.at[slot],
            recv_sem=recv_sem.at[slot],
            device_id=device,
            device_id_type=pl.DeviceIdType.MESH,
        )
        copy.start()
        return copy

    def piece_ref(index):
        return act if index == 0 else acts.at[index - 1]

    def lanes(index, size):
        return pl.ds(pl.multiple_of(index * size, size), size)

    barrier = pltpu.get_barrier_semaphore()
    friends = [at_col(bit) for bit in range(bits + 1)]
    friends += [((row + step) % rows, col) for step in range(1, rows)]
    for friend in friends:
        pl.semaphore_signal(
            barrier, inc=1, device_id=friend, device_id_type=pl.DeviceIdType.MESH
        )
    pl.semaphore_wait(barrier, len(friends))

    arrivals = {}

    def forward(index):
        for bit in range(1, bits + 1):
            if 1 << (bit - 1) > index:
                slot = (1 << (bit - 1)) + index
                arrivals[slot] = send(piece_ref(index), acts.at[slot - 1], at_col(bit))

    own_columns = lanes(side, width)
    sibling_og = send(
        og.at[lanes(1 - side, piece)], grads.at[row, :, own_columns], at_col(0)
    )
    kept = pltpu.make_async_copy(
        og.at[lanes(side, piece)], grads.at[row, :, own_columns], local_sem.at[0]
    )
    kept.start()
    forward(0)
    diag_copy = send(stat.at[:, lanes(half_index, half)], other_diag, at_col(1))
    kept.wait()
    sibling_og.wait()
    og_copies = [
        send(grads.at[row], grads.at[row], ((row + step) % rows, col)) for step in range(1, rows)
    ]

    own_max = jnp.max(
        jnp.sum(jnp.abs(stat[...]), axis=1, keepdims=True), axis=0, keepdims=True
    )
    eye = (
        lax.broadcasted_iota(jnp.int32, (half, half), 0)
        == lax.broadcasted_iota(jnp.int32, (half, half), 1)
    ).astype(F32)
    own_trace = total(stat[:, lanes(half_index, half)] * eye)

    def add_piece(index):
        source = col // 2
        for bit in range(bits):
            if index >> bit & 1:
                source = flip(source, bit)

        def rows_of(step, carry):
            here = lanes(step, block)
            term = product(piece_ref(index)[:, here], grads[source], ((0,), (0,)))
            if index == 0:
                partial[here, :] = term
            else:
                partial[here, :] += term
            return carry

        lax.fori_loop(0, order // block, rows_of, 0)

    for index in range(1, pieces):
        arrivals[index].wait_recv()
        forward(index)
    for copy in og_copies:
        copy.wait_recv()
    for index in range(pieces):
        add_piece(index)
    swap = send(partial.at[:, lanes(1 - side, width)], from_sibling, at_col(0))

    diag_copy.wait_recv()
    own_off = stat[:, lanes(1 - half_index, half)]
    far = other_diag[...]
    far_sums = jnp.sum(jnp.abs(own_off), axis=0, keepdims=True) + jnp.sum(
        jnp.abs(far), axis=0, keepdims=True
    )
    far_max = jnp.max(far_sums, axis=1, keepdims=True)
    damping = 10.0 ** (-DAMP_EXP) * (own_trace + total(far * eye)) / order
    scaling = (jnp.maximum(own_max, far_max) + damping) / 4.0
    scale = 0.25 / scaling
    shift = 1.25 - damping * scale
    top = shift * eye - stat[:, lanes(half_index, half)] * scale
    f_hi[:half, :half], f_lo[:half, :half] = split(top)
    off = -(own_off * scale)
    f_hi[:half, half:], f_lo[:half, half:] = split(off)
    f_hi[half:, :half], f_lo[half:, :half] = split(off.T)
    f_hi[half:, half:], f_lo[half:, half:] = split(shift * eye - far * scale)

    def triple(a_hi, a_lo, b_hi, b_lo, here):
        return (
            product(a_hi[here, :], b_hi[...])
            + product(a_hi[here, :], b_lo[...])
            + product(a_lo[here, :], b_hi[...])
        )

    def square_rows(step, carry):
        here = lanes(step, block)
        square = triple(f_hi, f_lo, f_hi, f_lo, here)
        q_hi[here, :], q_lo[here, :] = split(square)
        rest = 5.0 * (f_hi[here, :].astype(F32) + f_lo[here, :].astype(F32)) - 4.0 * square
        w_hi[here, :], w_lo[here, :] = split(rest)
        return carry

    lax.fori_loop(0, order // block, square_rows, 0)

    swap.wait_recv()
    tile = (partial[:, own_columns] + from_sibling[...]).astype(BF16)
    pair_own[:, own_columns] = tile
    tile_sibling = send(pair_own.at[:, own_columns], pair_own.at[:, own_columns], at_col(0))
    tile_far = send(pair_own.at[:, own_columns], pair_other.at[:, own_columns], at_col(1))

    def fourth_rows(step, carry):
        here = lanes(step, block)
        p_hi[here, :], p_lo[here, :] = split(triple(q_hi, q_lo, q_hi, q_lo, here))
        return carry

    lax.fori_loop(0, half // block, fourth_rows, 0)

    def root_rows(step, carry):
        here = lanes(step, block)
        value = 5.0 * (f_hi[here, :].astype(F32) + f_lo[here, :].astype(F32))
        value = (value - triple(p_hi, p_lo, w_hi, w_lo, here)) / 4.0
        root[here, :] = value.astype(BF16)
        return carry

    lax.fori_loop(0, half // block, root_rows, 0)
    root_copy = send(root, root_sibling, at_col(0))
    tile_far.wait_recv()
    far_sibling = send(pair_other.at[:, own_columns], pair_other.at[:, own_columns], at_col(0))
    root_copy.wait_recv()
    left[...] = jnp.where(side == 0, root[...], root_sibling[...])
    left_copy = send(left.at[:, pl.ds(0, half)], left_other, at_col(1))
    tile_sibling.wait_recv()
    far_sibling.wait_recv()

    fresh = (1.0 - DECAY) / order

    @pl.when(side == 0)
    def _():
        def gram_rows(step, carry):
            there = pl.ds(pl.multiple_of(half_index * half + step * block, block), block)
            here = lanes(step, block)
            gram = product(pair_own[there, :], pair_own[...], ((1,), (1,)))
            gram += product(pair_other[there, :], pair_other[...], ((1,), (1,)))
            renewed[here, :] = DECAY * stat[here, :] + fresh * gram
            return carry

        lax.fori_loop(0, half // block, gram_rows, 0)

    @pl.when(side == 1)
    def _():
        def gram_rows(step, carry):
            here = lanes(step, block)
            mine = pair_own[:, here]
            for position, pair in ((half_index, pair_own), (1 - half_index, pair_other)):
                there = lanes(position, half)
                gram = product(mine, pair[...], ((0,), (0,)))
                renewed[here, there] = DECAY * stat[here, there] + fresh * gram
            return carry

        lax.fori_loop(0, half // block, gram_rows, 0)

    right = jnp.where(side == 0, root_sibling[:width, :], root[half - width :, :])
    for place, natural in ((0, half_index), (1, 1 - half_index)):
        there = lanes(natural, half)
        value = product(pair_own[there, :], right[:, :half], ((1,), (1,)))
        value += product(pair_other[there, :], right[:, half:], ((1,), (1,)))
        hp[place * half : (place + 1) * half, :] = value.astype(BF16)
    cond_own = product(left[...], hp[...])
    cond_other = product(left[:, half:], hp[:half, :], ((0,), (0,)))
    left_copy.wait_recv()
    cond_other += product(left_other[...], hp[half:, :])
    values = pair_own[:, own_columns].astype(F32)
    count = order * width
    power = (total(cond_own * cond_own) + total(cond_other * cond_other)) / count
    ratio = jnp.sqrt(total(values * values) / count / (power + EPS))
    update[lanes(half_index, half), :] = (cond_own * ratio).astype(BF16)
    update[lanes(1 - half_index, half), :] = (cond_other * ratio).astype(BF16)

    everything = [list(arrivals.values()), og_copies]
    everything += [[diag_copy, swap, tile_sibling, tile_far, root_copy, far_sibling, left_copy]]
    for group in everything:
        for copy in group:
            copy.wait_send()


def local(rows, cols, activations, out_grads, statistics):
    stat = statistics[0, 0]
    half, order = stat.shape
    piece = activations.shape[0]
    width = out_grads.shape[1]
    pieces = cols // 2
    copies = pieces - 1 + rows - 1 + 8
    square = pltpu.VMEM((order, order), BF16)
    strip = pltpu.VMEM((half, order), BF16)
    pair = pltpu.VMEM((order, 2 * width), BF16)
    renewed, update = pl.pallas_call(
        functools.partial(shampoo_kernel, rows, cols),
        out_shape=(
            jax.ShapeDtypeStruct((half, order), F32),
            jax.ShapeDtypeStruct((order, width), BF16),
        ),
        in_specs=[pl.BlockSpec(memory_space=pltpu.VMEM)] * 3,
        out_specs=[pl.BlockSpec(memory_space=pltpu.VMEM)] * 2,
        scratch_shapes=[
            pltpu.VMEM((pieces - 1, piece, order), BF16),
            pltpu.VMEM((rows, piece, 2 * width), BF16),
            pltpu.VMEM((order, 2 * width), F32),
            pltpu.VMEM((order, width), F32),
            pair,
            pair,
            pltpu.VMEM((half, half), F32),
            square,
            square,
            square,
            square,
            square,
            square,
            strip,
            strip,
            strip,
            strip,
            strip,
            pltpu.VMEM((half, half), BF16),
            pltpu.VMEM((order, width), BF16),
            pltpu.SemaphoreType.DMA((copies,)),
            pltpu.SemaphoreType.DMA((copies,)),
            pltpu.SemaphoreType.DMA((1,)),
        ],
        compiler_params=pltpu.CompilerParams(
            collective_id=0, has_side_effects=True, vmem_limit_bytes=60 * 1024 * 1024
        ),
    )(activations, out_grads, stat)
    return (renewed[None, None], update)


def solution(mesh):
    placed = (P("col", "row"), P("row", "col"), P("row", "col", None, None))
    return jax.shard_map(
        functools.partial(local, mesh.shape["row"], mesh.shape["col"]),
        mesh=mesh,
        in_specs=placed,
        out_specs=(P("row", "col", None, None), P("row", "col")),
        check_vma=False,
    )
```

```python
import functools

import jax
import jax.numpy as jnp
from jax import lax
from jax.experimental import pallas as pl
from jax.experimental.pallas import tpu as pltpu
from jax.sharding import PartitionSpec as P

DAMP_EXP = 3
DECAY = 0.9
EPS = 1e-06

F32 = jnp.float32
BF16 = jnp.bfloat16


def product(left, right, over=((1,), (0,))):
    return lax.dot_general(left, right, (over, ((), ())), preferred_element_type=F32)


def split(value):
    high = value.astype(BF16)
    return high, (value - high.astype(F32)).astype(BF16)


def total(value):
    return jnp.sum(jnp.sum(value, axis=1, keepdims=True), axis=0, keepdims=True)


def flip(index, bit):
    return index + (1 - 2 * (index // (1 << bit) % 2)) * (1 << bit)


def shampoo_kernel(
    rows,
    cols,
    act,
    og,
    stat,
    renewed,
    update,
    acts,
    grads,
    partial,
    from_sibling,
    pair_own,
    pair_other,
    other_diag,
    f_hi,
    f_lo,
    q_hi,
    q_lo,
    w_hi,
    w_lo,
    p_hi,
    p_lo,
    root,
    root_sibling,
    left,
    left_other,
    hp,
    send_sem,
    recv_sem,
    local_sem,
):
    row = lax.axis_index("row")
    col = lax.axis_index("col")
    side = col % 2
    half_index = col // 2 % 2
    half, order = stat.shape
    piece = act.shape[0]
    width = og.shape[1]
    pieces = cols // 2
    bits = pieces.bit_length() - 1
    block = width
    used = [0]

    def at_col(bit):
        return (row, flip(col, bit))

    def remote(src, dst, device):
        slot = used[0]
        used[0] += 1
        return pltpu.make_async_remote_copy(
            src_ref=src,
            dst_ref=dst,
            send_sem=send_sem.at[slot],
            recv_sem=recv_sem.at[slot],
            device_id=device,
            device_id_type=pl.DeviceIdType.MESH,
        )

    def send(src, dst, device):
        copy = remote(src, dst, device)
        copy.start()
        return copy

    def piece_ref(index):
        return act if index == 0 else acts.at[index - 1]

    def lanes(index, size):
        return pl.ds(pl.multiple_of(index * size, size), size)

    barrier = pltpu.get_barrier_semaphore()
    friends = [at_col(bit) for bit in range(bits + 1)]
    friends += [((row + step) % rows, col) for step in range(1, rows)]
    for friend in friends:
        pl.semaphore_signal(
            barrier, inc=1, device_id=friend, device_id_type=pl.DeviceIdType.MESH
        )
    pl.semaphore_wait(barrier, len(friends))

    arrivals = {}

    def forward(index):
        for bit in range(1, bits + 1):
            if 1 << (bit - 1) > index:
                slot = (1 << (bit - 1)) + index
                arrivals[slot] = send(piece_ref(index), acts.at[slot - 1], at_col(bit))

    own_columns = lanes(side, width)
    sibling_og = send(
        og.at[lanes(1 - side, piece)], grads.at[row, :, own_columns], at_col(0)
    )
    kept = pltpu.make_async_copy(
        og.at[lanes(side, piece)], grads.at[row, :, own_columns], local_sem.at[0]
    )
    kept.start()
    forward(0)
    diag_copy = send(stat.at[:, lanes(half_index, half)], other_diag, at_col(1))
    kept.wait()
    sibling_og.wait()

    hops = []
    for hop in range(rows - 1):
        for sign in (1, -1):
            source = (row - sign * hop + rows) % rows
            target = (row + sign + rows) % rows
            copy = remote(grads.at[source], grads.at[source], (target, col))
            last = rows - 1 if sign == 1 else 0
            has_source = row - hop >= 0 if sign == 1 else row + hop < rows
            sends = jnp.logical_and(has_source, row != last)
            gets = row - 1 - hop >= 0 if sign == 1 else row + 1 + hop < rows
            hops.append((hop, copy, sends, gets))

    def start_hop(hop):
        for number, copy, sends, _ in hops:
            if number == hop:
                pl.when(sends)(copy.start)

    def wait_hop(hop):
        for number, copy, _, gets in hops:
            if number == hop:
                pl.when(gets)(copy.wait_recv)

    start_hop(0)

    own_max = jnp.max(
        jnp.sum(jnp.abs(stat[...]), axis=1, keepdims=True), axis=0, keepdims=True
    )
    eye = (
        lax.broadcasted_iota(jnp.int32, (half, half), 0)
        == lax.broadcasted_iota(jnp.int32, (half, half), 1)
    ).astype(F32)
    own_trace = total(stat[:, lanes(half_index, half)] * eye)

    def add_piece(index):
        source = col // 2
        for bit in range(bits):
            if index >> bit & 1:
                source = flip(source, bit)

        def rows_of(step, carry):
            here = lanes(step, block)
            term = product(piece_ref(index)[:, here], grads[source], ((0,), (0,)))
            if index == 0:
                partial[here, :] = term
            else:
                partial[here, :] += term
            return carry

        lax.fori_loop(0, order // block, rows_of, 0)

    early = pieces - 1
    for turn in range(max(early, rows)):
        if turn < rows - 1:
            wait_hop(turn)
            if turn + 1 < rows - 1:
                start_hop(turn + 1)
        if 1 <= turn + 1 < early:
            arrivals[turn + 1].wait_recv()
            forward(turn + 1)
    for index in range(pieces - 1):
        add_piece(index)
    arrivals[pieces - 1].wait_recv()
    add_piece(pieces - 1)
    swap = send(partial.at[:, lanes(1 - side, width)], from_sibling, at_col(0))

    diag_copy.wait_recv()
    own_off = stat[:, lanes(1 - half_index, half)]
    far = other_diag[...]
    far_sums = jnp.sum(jnp.abs(own_off), axis=0, keepdims=True) + jnp.sum(
        jnp.abs(far), axis=0, keepdims=True
    )
    far_max = jnp.max(far_sums, axis=1, keepdims=True)
    damping = 10.0 ** (-DAMP_EXP) * (own_trace + total(far * eye)) / order
    scaling = (jnp.maximum(own_max, far_max) + damping) / 4.0
    scale = 0.25 / scaling
    shift = 1.25 - damping * scale
    top = shift * eye - stat[:, lanes(half_index, half)] * scale
    f_hi[:half, :half], f_lo[:half, :half] = split(top)
    off = -(own_off * scale)
    f_hi[:half, half:], f_lo[:half, half:] = split(off)
    f_hi[half:, :half], f_lo[half:, :half] = split(off.T)
    f_hi[half:, half:], f_lo[half:, half:] = split(shift * eye - far * scale)

    def triple(a_hi, a_lo, b_hi, b_lo, here):
        return (
            product(a_hi[here, :], b_hi[...])
            + product(a_hi[here, :], b_lo[...])
            + product(a_lo[here, :], b_hi[...])
        )

    def square_rows(step, carry):
        here = lanes(step, block)
        square = triple(f_hi, f_lo, f_hi, f_lo, here)
        q_hi[here, :], q_lo[here, :] = split(square)
        rest = 5.0 * (f_hi[here, :].astype(F32) + f_lo[here, :].astype(F32)) - 4.0 * square
        w_hi[here, :], w_lo[here, :] = split(rest)
        return carry

    lax.fori_loop(0, half // block, square_rows, 0)
    swap.wait_recv()
    tile = (partial[:, own_columns] + from_sibling[...]).astype(BF16)
    pair_own[:, own_columns] = tile
    tile_sibling = send(pair_own.at[:, own_columns], pair_own.at[:, own_columns], at_col(0))
    tile_far = send(pair_own.at[:, own_columns], pair_other.at[:, own_columns], at_col(1))

    lax.fori_loop(half // block, order // block, square_rows, 0)

    def fourth_rows(step, carry):
        here = lanes(step, block)
        p_hi[here, :], p_lo[here, :] = split(triple(q_hi, q_lo, q_hi, q_lo, here))
        return carry

    lax.fori_loop(0, half // block, fourth_rows, 0)

    blocks = half // block
    to_sibling, to_far, handed = [], [], []
    for step in range(blocks):
        here = pl.ds(step * block, block)
        value = 5.0 * (f_hi[here, :].astype(F32) + f_lo[here, :].astype(F32))
        value = (value - triple(p_hi, p_lo, w_hi, w_lo, here)) / 4.0
        root[here, :] = value.astype(BF16)
        quarter = left_other.at[here, :]
        to_sibling.append(remote(root.at[here, :], root_sibling.at[here, :], at_col(0)))
        to_far.append(remote(root.at[here, pl.ds(0, half)], quarter, at_col(1)))
        handed.append(remote(quarter, quarter, at_col(0)))

        if step == 0:
            to_sibling[step].start()
        else:
            pl.when(side == 0)(to_sibling[step].start)
        pl.when(side == 0)(to_far[step].start)

    fresh = (1.0 - DECAY) / order

    def gram_part(pair, position, first):
        def left_rows(step, carry):
            there = pl.ds(pl.multiple_of(half_index * half + step * block, block), block)
            here = lanes(step, block)
            gram = fresh * product(pair[there, :], pair[...], ((1,), (1,)))
            if first:
                renewed[here, :] = DECAY * stat[here, :] + gram
            else:
                renewed[here, :] += gram
            return carry

        def right_rows(step, carry):
            here = lanes(step, block)
            there = lanes(position, half)
            gram = product(pair_own[:, here], pair[...], ((0,), (0,)))
            renewed[here, there] = DECAY * stat[here, there] + fresh * gram
            return carry

        @pl.when(side == 0)
        def _():
            lax.fori_loop(0, blocks, left_rows, 0)

        @pl.when(side == 1)
        def _():
            lax.fori_loop(0, blocks, right_rows, 0)

    tile_sibling.wait_recv()
    gram_part(pair_own, half_index, True)
    tile_far.wait_recv()
    far_sibling = send(pair_other.at[:, own_columns], pair_other.at[:, own_columns], at_col(0))
    for step in range(blocks):
        if step == 0:
            to_sibling[step].wait_recv()

        @pl.when(side == 0)
        def _():
            to_far[step].wait_recv()
            handed[step].start()

    @pl.when(side == 0)
    def _():
        left[...] = root[...]

    @pl.when(side == 1)
    def _():
        for copy in to_sibling[1:]:
            copy.wait_recv()
        left[...] = root_sibling[...]

    far_sibling.wait_recv()
    gram_part(pair_other, 1 - half_index, False)

    right = jnp.where(side == 0, root_sibling[:width, :], root[half - width :, :])
    for place, natural in ((0, half_index), (1, 1 - half_index)):
        there = lanes(natural, half)
        value = product(pair_own[there, :], right[:, :half], ((1,), (1,)))
        value += product(pair_other[there, :], right[:, half:], ((1,), (1,)))
        hp[place * half : (place + 1) * half, :] = value.astype(BF16)
    cond_own = product(left[...], hp[...])
    cond_other = product(left[:, half:], hp[:half, :], ((0,), (0,)))

    @pl.when(side == 1)
    def _():
        for copy in handed:
            copy.wait_recv()

    cond_other += product(left_other[...], hp[half:, :])
    values = pair_own[:, own_columns].astype(F32)
    count = order * width
    power = (total(cond_own * cond_own) + total(cond_other * cond_other)) / count
    ratio = jnp.sqrt(total(values * values) / count / (power + EPS))
    update[lanes(half_index, half), :] = (cond_own * ratio).astype(BF16)
    update[lanes(1 - half_index, half), :] = (cond_other * ratio).astype(BF16)

    everything = list(arrivals.values())
    everything += [diag_copy, swap, tile_sibling, tile_far, far_sibling, to_sibling[0]]
    for copy in everything:
        copy.wait_send()
    for _, copy, sends, _ in hops:
        pl.when(sends)(copy.wait_send)

    @pl.when(side == 0)
    def _():
        for copy in to_sibling[1:] + to_far + handed:
            copy.wait_send()


def local(rows, cols, activations, out_grads, statistics):
    stat = statistics[0, 0]
    half, order = stat.shape
    piece = activations.shape[0]
    width = out_grads.shape[1]
    pieces = cols // 2
    copies = pieces - 1 + 2 * (rows - 1) + 6 + 3 * (half // width)
    square = pltpu.VMEM((order, order), BF16)
    strip = pltpu.VMEM((half, order), BF16)
    pair = pltpu.VMEM((order, 2 * width), BF16)
    renewed, update = pl.pallas_call(
        functools.partial(shampoo_kernel, rows, cols),
        out_shape=(
            jax.ShapeDtypeStruct((half, order), F32),
            jax.ShapeDtypeStruct((order, width), BF16),
        ),
        in_specs=[pl.BlockSpec(memory_space=pltpu.VMEM)] * 3,
        out_specs=[pl.BlockSpec(memory_space=pltpu.VMEM)] * 2,
        scratch_shapes=[
            pltpu.VMEM((pieces - 1, piece, order), BF16),
            pltpu.VMEM((rows, piece, 2 * width), BF16),
            pltpu.VMEM((order, 2 * width), F32),
            pltpu.VMEM((order, width), F32),
            pair,
            pair,
            pltpu.VMEM((half, half), F32),
            square,
            square,
            square,
            square,
            square,
            square,
            strip,
            strip,
            strip,
            strip,
            strip,
            pltpu.VMEM((half, half), BF16),
            pltpu.VMEM((order, width), BF16),
            pltpu.SemaphoreType.DMA((copies,)),
            pltpu.SemaphoreType.DMA((copies,)),
            pltpu.SemaphoreType.DMA((1,)),
        ],
        compiler_params=pltpu.CompilerParams(
            collective_id=0, has_side_effects=True, vmem_limit_bytes=60 * 1024 * 1024
        ),
    )(activations, out_grads, stat)
    return (renewed[None, None], update)


def solution(mesh):
    placed = (P("col", "row"), P("row", "col"), P("row", "col", None, None))
    return jax.shard_map(
        functools.partial(local, mesh.shape["row"], mesh.shape["col"]),
        mesh=mesh,
        in_specs=placed,
        out_specs=(P("row", "col", None, None), P("row", "col")),
        check_vma=False,
    )
```

```python
import functools

import jax
import jax.numpy as jnp
from jax import lax
from jax.experimental import pallas as pl
from jax.experimental.pallas import tpu as pltpu
from jax.sharding import PartitionSpec as P

DAMP_EXP = 3
DECAY = 0.9
EPS = 1e-06

F32 = jnp.float32
BF16 = jnp.bfloat16


def product(left, right, over=((1,), (0,))):
    return lax.dot_general(left, right, (over, ((), ())), preferred_element_type=F32)


def split(value):
    high = value.astype(BF16)
    return high, (value - high.astype(F32)).astype(BF16)


def total(value):
    return jnp.sum(jnp.sum(value, axis=1, keepdims=True), axis=0, keepdims=True)


def flip(index, bit):
    return index + (1 - 2 * (index // (1 << bit) % 2)) * (1 << bit)


def shampoo_kernel(
    rows,
    cols,
    act,
    og,
    stat,
    renewed,
    update,
    acts,
    grads,
    partial,
    from_sibling,
    pair_own,
    pair_other,
    other_diag,
    f_hi,
    f_lo,
    q_hi,
    q_lo,
    w_hi,
    w_lo,
    p_hi,
    p_lo,
    root,
    root_sibling,
    left,
    left_other,
    hp,
    facts,
    far_facts,
    squares,
    send_sem,
    recv_sem,
    local_sem,
):
    row = lax.axis_index("row")
    col = lax.axis_index("col")
    side = col % 2
    half_index = col // 2 % 2
    half, order = stat.shape
    piece = act.shape[0]
    width = og.shape[1]
    pieces = cols // 2
    bits = pieces.bit_length() - 1
    block = width
    used = [0]

    def at_col(bit):
        return (row, flip(col, bit))

    def remote(src, dst, device):
        slot = used[0]
        used[0] += 1
        return pltpu.make_async_remote_copy(
            src_ref=src,
            dst_ref=dst,
            send_sem=send_sem.at[slot],
            recv_sem=recv_sem.at[slot],
            device_id=device,
            device_id_type=pl.DeviceIdType.MESH,
        )

    def send(src, dst, device):
        copy = remote(src, dst, device)
        copy.start()
        return copy

    def piece_ref(index):
        return act if index == 0 else acts.at[index - 1]

    def lanes(index, size):
        return pl.ds(pl.multiple_of(index * size, size), size)

    barrier = pltpu.get_barrier_semaphore()
    friends = [at_col(bit) for bit in range(bits + 1)]
    friends += [((row + step) % rows, col) for step in range(1, rows)]
    for friend in friends:
        pl.semaphore_signal(
            barrier, inc=1, device_id=friend, device_id_type=pl.DeviceIdType.MESH
        )
    pl.semaphore_wait(barrier, len(friends))

    arrivals = {}

    def forward(index):
        for bit in range(1, bits + 1):
            if 1 << (bit - 1) > index:
                slot = (1 << (bit - 1)) + index
                arrivals[slot] = send(piece_ref(index), acts.at[slot - 1], at_col(bit))

    own_columns = lanes(side, width)
    sibling_og = send(
        og.at[lanes(1 - side, piece)], grads.at[row, :, own_columns], at_col(0)
    )
    kept = pltpu.make_async_copy(
        og.at[lanes(side, piece)], grads.at[row, :, own_columns], local_sem.at[0]
    )
    kept.start()
    forward(0)
    kept.wait()
    sibling_og.wait()

    hops = []
    for hop in range(rows - 1):
        for sign in (1, -1):
            source = (row - sign * hop + rows) % rows
            target = (row + sign + rows) % rows
            copy = remote(grads.at[source], grads.at[source], (target, col))
            last = rows - 1 if sign == 1 else 0
            has_source = row - hop >= 0 if sign == 1 else row + hop < rows
            sends = jnp.logical_and(has_source, row != last)
            gets = row - 1 - hop >= 0 if sign == 1 else row + 1 + hop < rows
            hops.append((hop, copy, sends, gets))

    def start_hop(hop):
        for number, copy, sends, _ in hops:
            if number == hop:
                pl.when(sends)(copy.start)

    def wait_hop(hop):
        for number, copy, _, gets in hops:
            if number == hop:
                pl.when(gets)(copy.wait_recv)

    start_hop(0)

    own_max = jnp.max(
        jnp.sum(jnp.abs(stat[...]), axis=1, keepdims=True), axis=0, keepdims=True
    )
    eye = (
        lax.broadcasted_iota(jnp.int32, (half, half), 0)
        == lax.broadcasted_iota(jnp.int32, (half, half), 1)
    ).astype(F32)
    own_trace = total(stat[:, lanes(half_index, half)] * eye)
    facts[0:1, :] = jnp.broadcast_to(own_max, (1, 128))
    facts[1:2, :] = jnp.broadcast_to(own_trace, (1, 128))
    facts[2:8, :] = jnp.zeros((6, 128), F32)
    facts_copy = send(facts, far_facts, at_col(1))
    diag_copy = send(stat.at[:, lanes(half_index, half)], other_diag, at_col(1))

    def add_piece(index, first, last):
        source = col // 2
        for bit in range(bits):
            if index >> bit & 1:
                source = flip(source, bit)

        def rows_of(step, carry):
            here = lanes(step, block)
            term = product(piece_ref(index)[:, here], grads[source], ((0,), (0,)))
            if index == 0:
                partial[here, :] = term
            else:
                partial[here, :] += term
            return carry

        lax.fori_loop(first, last, rows_of, 0)

    def triple(a_hi, a_lo, b_hi, b_lo, here, along=slice(None)):
        return (
            product(a_hi[here, along], b_hi[along, :])
            + product(a_hi[here, along], b_lo[along, :])
            + product(a_lo[here, along], b_hi[along, :])
        )

    def prepare():
        facts_copy.wait_recv()
        trace = own_trace + far_facts[1:2, 0:1]
        damping = 10.0 ** (-DAMP_EXP) * trace / order
        scaling = (jnp.maximum(own_max, far_facts[0:1, 0:1]) + damping) / 4.0
        scale = 0.25 / scaling
        shift = 1.25 - damping * scale
        top = shift * eye - stat[:, lanes(half_index, half)] * scale
        f_hi[:half, :half], f_lo[:half, :half] = split(top)
        off = -(stat[:, lanes(1 - half_index, half)] * scale)
        f_hi[:half, half:], f_lo[:half, half:] = split(off)
        f_hi[half:, :half], f_lo[half:, :half] = split(off.T)

        def near_rows(step, carry):
            here = lanes(step, block)
            squares[here, :] = triple(f_hi, f_lo, f_hi, f_lo, here, slice(0, half))
            return carry

        lax.fori_loop(0, order // block, near_rows, 0)
        return scale, shift

    early = pieces - 1
    for turn in range(max(early, rows)):
        if turn < rows - 1:
            wait_hop(turn)
            if turn + 1 < rows - 1:
                start_hop(turn + 1)
        if 1 <= turn + 1 < early:
            arrivals[turn + 1].wait_recv()
            forward(turn + 1)
        if turn == 1:
            scale, shift = prepare()
    for index in range(pieces - 1):
        add_piece(index, 0, order // block)
    arrivals[pieces - 1].wait_recv()
    blocks = half // block
    swaps = []
    for chunk in range(2):
        add_piece(pieces - 1, chunk * blocks, (chunk + 1) * blocks)
        strip = pl.ds(chunk * half, half)
        swaps.append(
            send(
                partial.at[strip, lanes(1 - side, width)], from_sibling.at[strip, :], at_col(0)
            )
        )

    diag_copy.wait_recv()
    f_hi[half:, half:], f_lo[half:, half:] = split(shift * eye - other_diag[...] * scale)

    def square_rows(step, carry):
        here = lanes(step, block)
        square = squares[here, :]
        square += triple(f_hi, f_lo, f_hi, f_lo, here, slice(half, order))
        q_hi[here, :], q_lo[here, :] = split(square)
        rest = 5.0 * (f_hi[here, :].astype(F32) + f_lo[here, :].astype(F32)) - 4.0 * square
        w_hi[here, :], w_lo[here, :] = split(rest)
        return carry

    tile_sibling, tile_far, far_sibling = [], [], []
    for chunk in range(2):
        lax.fori_loop(chunk, chunk + 1, square_rows, 0)
        strip = pl.ds(chunk * half, half)
        swaps[chunk].wait_recv()
        tile = (partial[strip, own_columns] + from_sibling[strip, :]).astype(BF16)
        pair_own[strip, own_columns] = tile
        mine = pair_own.at[strip, own_columns]
        there = pair_other.at[strip, own_columns]
        tile_far.append(send(mine, there, at_col(1)))
        tile_sibling.append(send(mine, mine, at_col(0)))
        far_sibling.append(remote(there, there, at_col(0)))
    lax.fori_loop(2, order // block, square_rows, 0)

    def fourth_rows(step, carry):
        here = lanes(step, block)
        p_hi[here, :], p_lo[here, :] = split(triple(q_hi, q_lo, q_hi, q_lo, here))
        return carry

    lax.fori_loop(0, half // block, fourth_rows, 0)

    to_sibling, to_far, handed = [], [], []
    for step in range(blocks):
        here = pl.ds(step * block, block)
        value = 5.0 * (f_hi[here, :].astype(F32) + f_lo[here, :].astype(F32))
        value = (value - triple(p_hi, p_lo, w_hi, w_lo, here)) / 4.0
        root[here, :] = value.astype(BF16)
        quarter = left_other.at[here, :]
        to_sibling.append(remote(root.at[here, :], root_sibling.at[here, :], at_col(0)))
        to_far.append(remote(root.at[here, pl.ds(0, half)], quarter, at_col(1)))
        handed.append(remote(quarter, quarter, at_col(0)))

        if step == 0:
            to_sibling[step].start()
        else:
            pl.when(side == 0)(to_sibling[step].start)
        pl.when(side == 0)(to_far[step].start)

    fresh = (1.0 - DECAY) / order

    def gram_part(pair, position, first):
        def left_rows(step, carry):
            there = pl.ds(pl.multiple_of(half_index * half + step * block, block), block)
            here = lanes(step, block)
            gram = fresh * product(pair[there, :], pair[...], ((1,), (1,)))
            if first:
                renewed[here, :] = DECAY * stat[here, :] + gram
            else:
                renewed[here, :] += gram
            return carry

        def right_rows(step, carry):
            here = lanes(step, block)
            there = lanes(position, half)
            gram = product(pair_own[:, here], pair[...], ((0,), (0,)))
            renewed[here, there] = DECAY * stat[here, there] + fresh * gram
            return carry

        @pl.when(side == 0)
        def _():
            lax.fori_loop(0, blocks, left_rows, 0)

        @pl.when(side == 1)
        def _():
            lax.fori_loop(0, blocks, right_rows, 0)

    tile_far[0].wait_recv()
    far_sibling[0].start()
    for copy in tile_sibling:
        copy.wait_recv()
    gram_part(pair_own, half_index, True)
    tile_far[1].wait_recv()
    far_sibling[1].start()
    for step in range(blocks):
        if step == 0:
            to_sibling[step].wait_recv()

        @pl.when(side == 0)
        def _():
            to_far[step].wait_recv()
            handed[step].start()

    @pl.when(side == 0)
    def _():
        left[...] = root[...]

    @pl.when(side == 1)
    def _():
        for copy in to_sibling[1:]:
            copy.wait_recv()
        left[...] = root_sibling[...]

    for copy in far_sibling:
        copy.wait_recv()
    gram_part(pair_other, 1 - half_index, False)

    right = jnp.where(side == 0, root_sibling[:width, :], root[half - width :, :])
    for place, natural in ((0, half_index), (1, 1 - half_index)):
        there = lanes(natural, half)
        value = product(pair_own[there, :], right[:, :half], ((1,), (1,)))
        value += product(pair_other[there, :], right[:, half:], ((1,), (1,)))
        hp[place * half : (place + 1) * half, :] = value.astype(BF16)
    cond_own = product(left[...], hp[...])
    cond_other = product(left[:, half:], hp[:half, :], ((0,), (0,)))

    @pl.when(side == 1)
    def _():
        for copy in handed:
            copy.wait_recv()

    cond_other += product(left_other[...], hp[half:, :])
    values = pair_own[:, own_columns].astype(F32)
    count = order * width
    power = (total(cond_own * cond_own) + total(cond_other * cond_other)) / count
    ratio = jnp.sqrt(total(values * values) / count / (power + EPS))
    update[lanes(half_index, half), :] = (cond_own * ratio).astype(BF16)
    update[lanes(1 - half_index, half), :] = (cond_other * ratio).astype(BF16)

    everything = list(arrivals.values())
    everything += swaps + tile_sibling + tile_far + far_sibling
    everything += [diag_copy, facts_copy, to_sibling[0]]
    for copy in everything:
        copy.wait_send()
    for _, copy, sends, _ in hops:
        pl.when(sends)(copy.wait_send)

    @pl.when(side == 0)
    def _():
        for copy in to_sibling[1:] + to_far + handed:
            copy.wait_send()


def local(rows, cols, activations, out_grads, statistics):
    stat = statistics[0, 0]
    half, order = stat.shape
    piece = activations.shape[0]
    width = out_grads.shape[1]
    pieces = cols // 2
    copies = pieces - 1 + 2 * (rows - 1) + 11 + 3 * (half // width)
    square = pltpu.VMEM((order, order), BF16)
    strip = pltpu.VMEM((half, order), BF16)
    pair = pltpu.VMEM((order, 2 * width), BF16)
    renewed, update = pl.pallas_call(
        functools.partial(shampoo_kernel, rows, cols),
        out_shape=(
            jax.ShapeDtypeStruct((half, order), F32),
            jax.ShapeDtypeStruct((order, width), BF16),
        ),
        in_specs=[pl.BlockSpec(memory_space=pltpu.VMEM)] * 3,
        out_specs=[pl.BlockSpec(memory_space=pltpu.VMEM)] * 2,
        scratch_shapes=[
            pltpu.VMEM((pieces - 1, piece, order), BF16),
            pltpu.VMEM((rows, piece, 2 * width), BF16),
            pltpu.VMEM((order, 2 * width), F32),
            pltpu.VMEM((order, width), F32),
            pair,
            pair,
            pltpu.VMEM((half, half), F32),
            square,
            square,
            square,
            square,
            square,
            square,
            strip,
            strip,
            strip,
            strip,
            strip,
            pltpu.VMEM((half, half), BF16),
            pltpu.VMEM((order, width), BF16),
            pltpu.VMEM((8, 128), F32),
            pltpu.VMEM((8, 128), F32),
            pltpu.VMEM((order, order), F32),
            pltpu.SemaphoreType.DMA((copies,)),
            pltpu.SemaphoreType.DMA((copies,)),
            pltpu.SemaphoreType.DMA((1,)),
        ],
        compiler_params=pltpu.CompilerParams(
            collective_id=0, has_side_effects=True, vmem_limit_bytes=60 * 1024 * 1024
        ),
    )(activations, out_grads, stat)
    return (renewed[None, None], update)


def solution(mesh):
    placed = (P("col", "row"), P("row", "col"), P("row", "col", None, None))
    return jax.shard_map(
        functools.partial(local, mesh.shape["row"], mesh.shape["col"]),
        mesh=mesh,
        in_specs=placed,
        out_specs=(P("row", "col", None, None), P("row", "col")),
        check_vma=False,
    )
```

```python
import functools

import jax
import jax.numpy as jnp
from jax import lax
from jax.experimental import pallas as pl
from jax.experimental.pallas import tpu as pltpu
from jax.sharding import PartitionSpec as P

DAMP_EXP = 3
DECAY = 0.9
EPS = 1e-06

F32 = jnp.float32
BF16 = jnp.bfloat16


def product(left, right, over=((1,), (0,))):
    return lax.dot_general(left, right, (over, ((), ())), preferred_element_type=F32)


def split(value):
    high = value.astype(BF16)
    return high, (value - high.astype(F32)).astype(BF16)


def total(value):
    return jnp.sum(jnp.sum(value, axis=1, keepdims=True), axis=0, keepdims=True)


def flip(index, bit):
    return index + (1 - 2 * (index // (1 << bit) % 2)) * (1 << bit)


def shampoo_kernel(
    rows,
    cols,
    act,
    og,
    stat,
    renewed,
    update,
    acts,
    grads,
    partial,
    from_sibling,
    pair_own,
    pair_other,
    other_diag,
    f_hi,
    f_lo,
    q_hi,
    q_lo,
    w_hi,
    w_lo,
    p_hi,
    p_lo,
    root,
    root_sibling,
    left,
    left_other,
    hp,
    facts,
    far_facts,
    squares,
    send_sem,
    recv_sem,
    local_sem,
):
    row = lax.axis_index("row")
    col = lax.axis_index("col")
    side = col % 2
    half_index = col // 2 % 2
    half, order = stat.shape
    piece = act.shape[0]
    width = og.shape[1]
    pieces = cols // 2
    bits = pieces.bit_length() - 1
    block = width
    used = [0]

    def at_col(bit):
        return (row, flip(col, bit))

    def remote(src, dst, device):
        slot = used[0]
        used[0] += 1
        return pltpu.make_async_remote_copy(
            src_ref=src,
            dst_ref=dst,
            send_sem=send_sem.at[slot],
            recv_sem=recv_sem.at[slot],
            device_id=device,
            device_id_type=pl.DeviceIdType.MESH,
        )

    def send(src, dst, device):
        copy = remote(src, dst, device)
        copy.start()
        return copy

    def piece_ref(index):
        return act if index == 0 else acts.at[index - 1]

    def lanes(index, size):
        return pl.ds(pl.multiple_of(index * size, size), size)

    barrier = pltpu.get_barrier_semaphore()
    friends = [at_col(bit) for bit in range(bits + 1)]
    friends += [((row + step) % rows, col) for step in range(1, rows)]
    for friend in friends:
        pl.semaphore_signal(
            barrier, inc=1, device_id=friend, device_id_type=pl.DeviceIdType.MESH
        )
    pl.semaphore_wait(barrier, len(friends))

    arrivals = {}

    def forward(index):
        for bit in range(1, bits + 1):
            if 1 << (bit - 1) > index:
                slot = (1 << (bit - 1)) + index
                arrivals[slot] = send(piece_ref(index), acts.at[slot - 1], at_col(bit))

    own_columns = lanes(side, width)
    sibling_og = send(
        og.at[lanes(1 - side, piece)], grads.at[row, :, own_columns], at_col(0)
    )
    kept = pltpu.make_async_copy(
        og.at[lanes(side, piece)], grads.at[row, :, own_columns], local_sem.at[0]
    )
    kept.start()
    forward(0)
    kept.wait()
    sibling_og.wait()

    hops = []
    for hop in range(rows - 1):
        for sign in (1, -1):
            source = (row - sign * hop + rows) % rows
            target = (row + sign + rows) % rows
            copy = remote(grads.at[source], grads.at[source], (target, col))
            last = rows - 1 if sign == 1 else 0
            has_source = row - hop >= 0 if sign == 1 else row + hop < rows
            sends = jnp.logical_and(has_source, row != last)
            gets = row - 1 - hop >= 0 if sign == 1 else row + 1 + hop < rows
            hops.append((hop, copy, sends, gets))

    def start_hop(hop):
        for number, copy, sends, _ in hops:
            if number == hop:
                pl.when(sends)(copy.start)

    def wait_hop(hop):
        for number, copy, _, gets in hops:
            if number == hop:
                pl.when(gets)(copy.wait_recv)

    start_hop(0)

    own_max = jnp.max(
        jnp.sum(jnp.abs(stat[...]), axis=1, keepdims=True), axis=0, keepdims=True
    )
    eye = (
        lax.broadcasted_iota(jnp.int32, (half, half), 0)
        == lax.broadcasted_iota(jnp.int32, (half, half), 1)
    ).astype(F32)
    own_trace = total(stat[:, lanes(half_index, half)] * eye)
    facts[0:1, :] = jnp.broadcast_to(own_max, (1, 128))
    facts[1:2, :] = jnp.broadcast_to(own_trace, (1, 128))
    facts[2:8, :] = jnp.zeros((6, 128), F32)
    facts_copy = send(facts, far_facts, at_col(1))
    diag_copy = send(stat.at[:, lanes(half_index, half)], other_diag, at_col(1))

    def add_piece(index, first, last):
        source = col // 2
        for bit in range(bits):
            if index >> bit & 1:
                source = flip(source, bit)

        def rows_of(step, carry):
            here = lanes(step, block)
            term = product(piece_ref(index)[:, here], grads[source], ((0,), (0,)))
            if index == 0:
                partial[here, :] = term
            else:
                partial[here, :] += term
            return carry

        lax.fori_loop(first, last, rows_of, 0)

    def triple(a_hi, a_lo, b_hi, b_lo, here, along=slice(None)):
        return (
            product(a_hi[here, along], b_hi[along, :])
            + product(a_hi[here, along], b_lo[along, :])
            + product(a_lo[here, along], b_hi[along, :])
        )

    def prepare():
        facts_copy.wait_recv()
        trace = own_trace + far_facts[1:2, 0:1]
        damping = 10.0 ** (-DAMP_EXP) * trace / order
        scaling = (jnp.maximum(own_max, far_facts[0:1, 0:1]) + damping) / 4.0
        scale = 0.25 / scaling
        shift = 1.25 - damping * scale
        top = shift * eye - stat[:, lanes(half_index, half)] * scale
        f_hi[:half, :half], f_lo[:half, :half] = split(top)
        off = -(stat[:, lanes(1 - half_index, half)] * scale)
        f_hi[:half, half:], f_lo[:half, half:] = split(off)
        f_hi[half:, :half], f_lo[half:, :half] = split(off.T)

        def near_rows(step, carry):
            here = lanes(step, block)
            squares[here, :] = triple(f_hi, f_lo, f_hi, f_lo, here, slice(0, half))
            return carry

        lax.fori_loop(0, order // block, near_rows, 0)
        return scale, shift

    early = pieces - 1
    for turn in range(max(early, rows)):
        if turn < rows - 1:
            wait_hop(turn)
            if turn + 1 < rows - 1:
                start_hop(turn + 1)
        if 1 <= turn + 1 < early:
            arrivals[turn + 1].wait_recv()
            forward(turn + 1)
        if turn == 1:
            scale, shift = prepare()
    for index in range(pieces - 1):
        add_piece(index, 0, order // block)
    arrivals[pieces - 1].wait_recv()
    blocks = half // block
    swaps = []
    for chunk in range(2):
        add_piece(pieces - 1, chunk * blocks, (chunk + 1) * blocks)
        strip = pl.ds(chunk * half, half)
        swaps.append(
            send(
                partial.at[strip, lanes(1 - side, width)], from_sibling.at[strip, :], at_col(0)
            )
        )

    diag_copy.wait_recv()
    f_hi[half:, half:], f_lo[half:, half:] = split(shift * eye - other_diag[...] * scale)

    def square_rows(step, carry):
        here = lanes(step, block)
        square = squares[here, :]
        square += triple(f_hi, f_lo, f_hi, f_lo, here, slice(half, order))
        q_hi[here, :], q_lo[here, :] = split(square)
        rest = 5.0 * (f_hi[here, :].astype(F32) + f_lo[here, :].astype(F32)) - 4.0 * square
        w_hi[here, :], w_lo[here, :] = split(rest)
        return carry

    tile_sibling, tile_far, far_sibling = [], [], []
    for chunk in range(2):
        lax.fori_loop(chunk, chunk + 1, square_rows, 0)
        strip = pl.ds(chunk * half, half)
        swaps[chunk].wait_recv()
        tile = (partial[strip, own_columns] + from_sibling[strip, :]).astype(BF16)
        pair_own[strip, own_columns] = tile
        mine = pair_own.at[strip, own_columns]
        there = pair_other.at[strip, own_columns]
        tile_far.append(send(mine, there, at_col(1)))
        tile_sibling.append(send(mine, mine, at_col(0)))
        far_sibling.append(remote(there, there, at_col(0)))
    lax.fori_loop(2, order // block, square_rows, 0)

    def fourth_rows(step, carry):
        here = lanes(step, block)
        p_hi[here, :], p_lo[here, :] = split(triple(q_hi, q_lo, q_hi, q_lo, here))
        return carry

    lax.fori_loop(0, half // block, fourth_rows, 0)

    to_sibling, to_far, handed = [], [], []
    for step in range(blocks):
        here = pl.ds(step * block, block)
        value = 5.0 * (f_hi[here, :].astype(F32) + f_lo[here, :].astype(F32))
        value = (value - triple(p_hi, p_lo, w_hi, w_lo, here)) / 4.0
        root[here, :] = value.astype(BF16)
        quarter = left_other.at[here, :]
        to_sibling.append(remote(root.at[here, :], root_sibling.at[here, :], at_col(0)))
        to_far.append(remote(root.at[here, pl.ds(0, half)], quarter, at_col(1)))
        handed.append(remote(quarter, quarter, at_col(0)))

        if step == 0:
            to_sibling[step].start()
        else:
            pl.when(side == 0)(to_sibling[step].start)
        pl.when(side == 0)(to_far[step].start)

    fresh = (1.0 - DECAY) / order

    def gram_part(pair, position, first):
        def left_rows(step, carry):
            there = pl.ds(pl.multiple_of(half_index * half + step * block, block), block)
            here = lanes(step, block)
            gram = fresh * product(pair[there, :], pair[...], ((1,), (1,)))
            if first:
                renewed[here, :] = DECAY * stat[here, :] + gram
            else:
                renewed[here, :] += gram
            return carry

        def right_rows(step, carry):
            here = lanes(step, block)
            there = lanes(position, half)
            gram = product(pair_own[:, here], pair[...], ((0,), (0,)))
            renewed[here, there] = DECAY * stat[here, there] + fresh * gram
            return carry

        @pl.when(side == 0)
        def _():
            lax.fori_loop(0, blocks, left_rows, 0)

        @pl.when(side == 1)
        def _():
            lax.fori_loop(0, blocks, right_rows, 0)

    tile_far[0].wait_recv()
    far_sibling[0].start()
    for copy in tile_sibling:
        copy.wait_recv()
    gram_part(pair_own, half_index, True)
    tile_far[1].wait_recv()
    far_sibling[1].start()
    for step in range(blocks):
        if step == 0:
            to_sibling[step].wait_recv()

        @pl.when(side == 0)
        def _():
            to_far[step].wait_recv()
            handed[step].start()

    @pl.when(side == 0)
    def _():
        left[...] = root[...]

    @pl.when(side == 1)
    def _():
        for copy in to_sibling[1:]:
            copy.wait_recv()
        left[...] = root_sibling[...]

    for copy in far_sibling:
        copy.wait_recv()
    gram_part(pair_other, 1 - half_index, False)

    right = jnp.where(side == 0, root_sibling[:width, :], root[half - width :, :])
    for place, natural in ((0, half_index), (1, 1 - half_index)):
        there = lanes(natural, half)
        value = product(pair_own[there, :], right[:, :half], ((1,), (1,)))
        value += product(pair_other[there, :], right[:, half:], ((1,), (1,)))
        hp[place * half : (place + 1) * half, :] = value.astype(BF16)
    cond_own = product(left[...], hp[...])
    cond_other = product(left[:, half:], hp[:half, :], ((0,), (0,)))

    @pl.when(side == 1)
    def _():
        for copy in handed:
            copy.wait_recv()

    cond_other += product(left_other[...], hp[half:, :])
    values = pair_own[:, own_columns].astype(F32)
    count = order * width
    power = (total(cond_own * cond_own) + total(cond_other * cond_other)) / count
    ratio = jnp.sqrt(total(values * values) / count / (power + EPS))
    update[lanes(half_index, half), :] = (cond_own * ratio).astype(BF16)
    update[lanes(1 - half_index, half), :] = (cond_other * ratio).astype(BF16)

    everything = list(arrivals.values())
    everything += swaps + tile_sibling + tile_far + far_sibling
    everything += [diag_copy, facts_copy, to_sibling[0]]
    for copy in everything:
        copy.wait_send()
    for _, copy, sends, _ in hops:
        pl.when(sends)(copy.wait_send)

    @pl.when(side == 0)
    def _():
        for copy in to_sibling[1:] + to_far + handed:
            copy.wait_send()


def local(rows, cols, activations, out_grads, statistics):
    stat = statistics[0, 0]
    half, order = stat.shape
    piece = activations.shape[0]
    width = out_grads.shape[1]
    pieces = cols // 2
    copies = pieces - 1 + 2 * (rows - 1) + 11 + 3 * (half // width)
    square = pltpu.VMEM((order, order), BF16)
    strip = pltpu.VMEM((half, order), BF16)
    pair = pltpu.VMEM((order, 2 * width), BF16)
    renewed, update = pl.pallas_call(
        functools.partial(shampoo_kernel, rows, cols),
        out_shape=(
            jax.ShapeDtypeStruct((half, order), F32),
            jax.ShapeDtypeStruct((order, width), BF16),
        ),
        in_specs=[pl.BlockSpec(memory_space=pltpu.VMEM)] * 3,
        out_specs=[pl.BlockSpec(memory_space=pltpu.VMEM)] * 2,
        scratch_shapes=[
            pltpu.VMEM((pieces - 1, piece, order), BF16),
            pltpu.VMEM((rows, piece, 2 * width), BF16),
            pltpu.VMEM((order, 2 * width), F32),
            pltpu.VMEM((order, width), F32),
            pair,
            pair,
            pltpu.VMEM((half, half), F32),
            square,
            square,
            square,
            square,
            square,
            square,
            strip,
            strip,
            strip,
            strip,
            strip,
            pltpu.VMEM((half, half), BF16),
            pltpu.VMEM((order, width), BF16),
            pltpu.VMEM((8, 128), F32),
            pltpu.VMEM((8, 128), F32),
            pltpu.VMEM((order, order), F32),
            pltpu.SemaphoreType.DMA((copies,)),
            pltpu.SemaphoreType.DMA((copies,)),
            pltpu.SemaphoreType.DMA((1,)),
        ],
        compiler_params=pltpu.CompilerParams(
            collective_id=0, has_side_effects=True, vmem_limit_bytes=48 * 1024 * 1024
        ),
    )(activations, out_grads, stat)
    return (renewed[None, None], update)


def solution(mesh):
    placed = (P("col", "row"), P("row", "col"), P("row", "col", None, None))
    return jax.shard_map(
        functools.partial(local, mesh.shape["row"], mesh.shape["col"]),
        mesh=mesh,
        in_specs=placed,
        out_specs=(P("row", "col", None, None), P("row", "col")),
        check_vma=False,
    )
```
